32 devices in a mesh: cfd: 8 (over z, core), panel: 2 (over y), obs: 2 (over x).
Axes of the slice: x: 2, y: 2, z: 4, core: 2. Of those that a mesh axis runs over, the one named last changes fastest.
Arguments:
- state: float32 [5, 64, 32, 256], P(None, 'cfd', 'panel', 'obs'), may hold values from -6 to 6
- mean_speed: float32 [64, 32, 256], P('cfd', 'panel', 'obs'), may hold values from 0 to 0.9
- eddy_visc: float32 [64, 32, 256], P('cfd', 'panel', 'obs'), may hold values from 0.02 to 0.5
- panel_cell: int32 [8, 2, 2, 8, 4], P('cfd', 'panel', 'obs'), may hold values from 0 to 16383
- panel_count: int32 [8, 2, 2, 8], P('cfd', 'panel', 'obs'), may hold values from 0 to 4, as said below
- weights: bfloat16 [16, 2, 8, 4, 2, 2, 64], P(('cfd', 'panel'), None, None, None, None, 'obs'), may hold values from -1.5 to 1.5
- delays: int32 [16, 2, 8, 2, 1], P(('cfd', 'panel'), None, None, 'obs'), may hold values from 0 to 124
Outputs:
- flow_out: float32 [5, 64, 32, 256], P(None, 'cfd', 'panel', 'obs')
- observer_pressure: float32 [2, 64, 128], P('obs', ('cfd', 'panel'))
The draws below stay inside these ranges and needn't reach their ends.
Inputs may be any that keep to these rules, and one draw needn't show every extreme that they name: `panel_cell`: A flat cell index within one flow block of 8 x 16 x 128 cells. `panel_count`: in every flow block some destination shard gets all 4 slots, and for each pair of second and third block indices that is the same shard for all blocks along the first dimension.
All inputs are finite; a program needn't handle non-finite values.
Results may differ from the reference program's by a relative error of at most 0.0029.
Values may be sent and summed in bfloat16 or wider, within the bound.
A program may use at most 64 MiB of HBM per device.

```python
import math
import jax
import jax.numpy as jnp
from jax import lax

CX = 8
CY = 16
CZ = 128
STEPS = 4
CAP = 4
NB = 128
NX = 64
NY = 32
NZ = 256
OBS_HALF = 64
OBS_BLOCK = 64
NBLK = 1
N_CFD = 8
N_PANEL = 2
N_OBS = 2


def draw_panel_count(key, part):
    key_base = jax.random.fold_in(key, 11)
    key_star = jax.random.fold_in(key, 12)
    shape_all = (N_CFD, N_PANEL, N_OBS, N_CFD)
    base = jax.random.randint(key_base, shape_all, 0, CAP + 1)
    star = jax.random.randint(key_star, (1, N_PANEL, N_OBS, 1), 0, N_CFD)
    destination = lax.broadcasted_iota(jnp.int32, shape_all, 3)
    return jnp.where(destination == star, CAP, base).astype(jnp.int32)


def with_ends(drawn, own_key, smallest, top_value):
    spot = [jax.random.randint(jax.random.fold_in(own_key, axis), (), 0, length) for axis, length in enumerate(drawn.shape)]
    longest = drawn.shape.index(max(drawn.shape))
    neighbour = spot[:longest] + [(spot[longest] + 1) % drawn.shape[longest]] + spot[longest + 1:]
    return drawn.at[tuple(spot)].set(smallest).at[tuple(neighbour)].set(top_value)


def strengthened(entries, stream_key, source, target, parts, factor):
    owner, partner = [(jnp.arange(entries.shape[dim]) // (entries.shape[dim] // parts)).reshape([-1 if axis == dim else 1 for axis in range(entries.ndim)]) for dim in (source, target)]
    chosen = jax.random.permutation(stream_key, parts)[partner]
    strong = (owner == chosen) | (owner == (partner + parts // 2) % parts)
    return jnp.where(strong, factor * entries, entries)


def shard_levels(stream_key, shape, shards, smallest, high):
    def one(dim, blocks):
        draws = jax.random.uniform(jax.random.fold_in(jax.random.fold_in(stream_key, 6), dim), (blocks,), jnp.float32, smallest / len(shards), high / len(shards))
        return jnp.repeat(jnp.exp(draws), shape[dim] // blocks).reshape((-1,) + (1,) * (len(shape) - dim - 1))

    gain = one(*shards[0])
    for cut in shards[1:]:
        gain = gain * one(*cut)
    return gain


def noise(rng, shape, scale, bound, shards=(), kind=jnp.bfloat16):
    level = shard_levels(rng, shape, shards, -0.22, 0.18) if shards else 1.0
    values = jax.random.normal(rng, shape, jnp.float32) * scale * level
    return jnp.minimum(jnp.maximum(values, -bound), bound).astype(kind)


def noise_with(rng, dims, scale, most, split, heavy, kind=jnp.bfloat16):
    array = scale * jax.random.normal(rng, dims, jnp.float32)
    if split:
        array = array * shard_levels(rng, dims, split, -0.22, 0.18)
    return jnp.clip(strengthened(array, jax.random.fold_in(rng, 3), *heavy), -most, most).astype(kind)


def setup_inputs(seed: int = 0) -> dict:
    key_of = jax.random.split(jax.random.key(seed), 8)
    return {
        "state": noise(key_of[0], (5, NX, NY, NZ), 1.0, 6.0, ((1, 8), (2, 2), (3, 2)), jnp.float32),
        "mean_speed": jnp.clip(0.9 * jax.random.uniform(key_of[1], (NX, NY, NZ), jnp.float32) ** shard_levels(key_of[1], (NX, NY, NZ), ((0, 8), (1, 2), (2, 2)), -0.2, 0.2), 0.0, 0.9),
        "eddy_visc": jnp.clip(jnp.exp(math.log(0.5) - 3.218876 * jax.random.uniform(key_of[2], (NX, NY, NZ), jnp.float32) ** shard_levels(key_of[2], (NX, NY, NZ), ((0, 8), (1, 2), (2, 2)), -0.2, 0.2)), 0.02, 0.5),
        "panel_cell": with_ends(jax.random.randint(key_of[3], (N_CFD, N_PANEL, N_OBS, N_CFD, CAP), 0, CX * CY * CZ), jax.random.fold_in(key_of[3], 1), 0, (CX * CY * CZ) - 1).astype(jnp.int32),
        "panel_count": draw_panel_count(jax.random.fold_in(key_of[7], 71), 0),
        "weights": noise_with(key_of[5], (N_CFD * N_PANEL, N_OBS, N_CFD, CAP, 2, N_OBS, OBS_HALF), (CAP * N_CFD * N_CFD * N_PANEL * N_OBS * STEPS // NB) ** -0.5, 1.5, ((0, 16), (5, 2)), (0, 6, 16, 2.0)),
        "delays": with_ends(jax.random.randint(key_of[6], (N_CFD * N_PANEL, N_OBS, N_CFD, N_OBS, NBLK), 0, NB - 3), jax.random.fold_in(key_of[6], 1), 0, (NB - 3) - 1).astype(jnp.int32),
    }


time_step = 0.2


def tendency(padded, flow_speed, viscosity):
    center = padded[:, 1:-1, 1:-1, 1:-1]
    east_side = padded[:, 2:, 1:-1, 1:-1]
    west_side = padded[:, :-2, 1:-1, 1:-1]
    north_side = padded[:, 1:-1, 2:, 1:-1]
    south_side = padded[:, 1:-1, :-2, 1:-1]
    upper_side = padded[:, 1:-1, 1:-1, 2:]
    lower_side = padded[:, 1:-1, 1:-1, :-2]
    along_x = 0.5 * (east_side - west_side)
    along_y = 0.5 * (north_side - south_side)
    along_z = 0.5 * (upper_side - lower_side)
    spread = east_side + west_side + north_side + south_side + upper_side + lower_side - 6.0 * center
    diverge = along_x[1] + along_y[2] + along_z[3]
    forcing = jnp.stack([diverge, along_x[4], along_y[4], along_z[4], diverge])
    return viscosity[None] * spread - flow_speed[None] * along_x - forcing


def pad_zero(fields):
    return jnp.pad(fields, ((0, 0), (1, 1), (1, 1), (1, 1)))


def advance(fields, flow_speed, viscosity, padder):
    first_section = fields + time_step * tendency(padder(fields), flow_speed, viscosity)
    second_section = 0.75 * fields + 0.25 * (first_section + time_step * tendency(padder(first_section), flow_speed, viscosity))
    return fields / 3.0 + (2.0 / 3.0) * (second_section + time_step * tendency(padder(second_section), flow_speed, viscosity))


def shard_sum(total, pieces):
    weight_block, signal_block, delay_block = pieces
    heard_now = jnp.einsum('zcjtho,zcjtk->hzcko', weight_block.astype(jnp.float32), signal_block.astype(jnp.float32), precision=lax.Precision.HIGHEST)
    heard_now = heard_now.reshape(N_OBS, N_OBS, N_CFD, STEPS, NBLK, OBS_BLOCK)
    target = jnp.transpose(delay_block, (2, 0, 1, 3))[..., None] + jnp.arange(STEPS, dtype=jnp.int32)
    onehot = (target[..., None] == jnp.arange(NB, dtype=jnp.int32)).astype(jnp.float32)
    placed = jnp.einsum('hzckbo,hzcbkn->hbon', heard_now, onehot, precision=lax.Precision.HIGHEST)
    return total + placed.reshape(N_OBS, OBS_HALF, NB), None


def reference(state, mean_speed, eddy_visc, panel_cell, panel_count, weights, delays):
    block_x = lax.broadcasted_iota(jnp.int32, panel_cell.shape, 0)
    block_y = lax.broadcasted_iota(jnp.int32, panel_cell.shape, 1)
    block_z = lax.broadcasted_iota(jnp.int32, panel_cell.shape, 2)
    row_x = block_x * CX + panel_cell // (CY * CZ)
    row_y = block_y * CY + (panel_cell // CZ) % CY
    row_z = block_z * CZ + panel_cell % CZ
    live_mask = (lax.broadcasted_iota(jnp.int32, panel_cell.shape, 4) < panel_count[..., None]).astype(jnp.float32)
    fields = state
    samples = []
    for counter in range(STEPS):
        fields = advance(fields, mean_speed, eddy_visc, pad_zero)
        density = fields[0][row_x, row_y, row_z]
        pressure = fields[4][row_x, row_y, row_z]
        samples.append((jnp.stack([density, pressure], axis=-1) * live_mask[..., None]).astype(jnp.bfloat16))
    signal = jnp.stack(samples, axis=-1)
    signal = jnp.transpose(signal, (3, 1, 2, 0, 4, 5, 6)).reshape(N_CFD * N_PANEL, N_OBS, N_CFD, CAP, 2, STEPS)
    start = jnp.zeros((N_OBS, OBS_HALF, NB), jnp.float32)
    pressure_out, unused = lax.scan(shard_sum, start, (weights, signal, delays))
    return fields, pressure_out
```

```python
import functools

import jax
import jax.numpy as jnp
from jax import lax
from jax.experimental import pallas as pl
from jax.experimental.pallas import tpu as pltpu
from jax.sharding import PartitionSpec as P

STEPS = 4
TIME_STEP = 0.2
PAD = 8
AXES = ("cfd", "panel", "obs")


def window_kernel(
    sizes,
    cells,
    counts,
    late_bins,
    state,
    speed,
    visc,
    weights,
    flow_out,
    heard_out,
    s_ref,
    hx_ref,
    hy_ref,
    ys_ref,
    m_ref,
    v_ref,
    vy_ref,
    vz_ref,
    zs_ref,
    zr_ref,
    raw_ref,
    g_ref,
    hot_ref,
    sig_ref,
    parcel_ref,
    w_ref,
    wt_ref,
    late_ref,
    early_ref,
    part_ref,
    gather_ref,
    load_sem,
    send_sem,
    recv_sem,
    w_sem,
    r_sem,
):
    span = dict(zip(AXES, sizes))
    cx, cy, cz = speed.shape
    rows = cx * cy
    me = {axis: lax.axis_index(axis) for axis in AXES}
    has = {}
    for axis in AXES:
        has[axis, 1] = me[axis] < span[axis] - 1
        has[axis, -1] = me[axis] > 0
    total = sizes[0] * sizes[1] * sizes[2]
    assert sizes[2] == 2
    low = me["obs"] > 0
    near = sum(sizes) - 3 <= 3 * (STEPS - 1)

    loads = [
        pltpu.make_async_copy(
            state, s_ref.at[0, :, :, pl.ds(PAD, cy), :], load_sem.at[0]
        ),
        pltpu.make_async_copy(speed, m_ref, load_sem.at[1]),
        pltpu.make_async_copy(visc, v_ref, load_sem.at[2]),
        pltpu.make_async_copy(weights, raw_ref, load_sem.at[3]),
    ]
    for load in loads:
        load.start()

    def place(index):
        return {
            "cfd": index // (sizes[1] * sizes[2]),
            "panel": (index // sizes[2]) % sizes[1],
            "obs": index % sizes[2],
        }

    my_index = (me["cfd"] * sizes[1] + me["panel"]) * sizes[2] + me["obs"]
    barrier = pltpu.get_barrier_semaphore()
    if near:
        met = jnp.int32(0)
        for axis in AXES:
            for way in (1, -1):

                @pl.when(has[axis, way])
                def _():
                    pl.semaphore_signal(
                        barrier,
                        inc=1,
                        device_id={**me, axis: me[axis] + way},
                        device_id_type=pl.DeviceIdType.MESH,
                    )

                met = met + has[axis, way].astype(jnp.int32)
        pl.semaphore_wait(barrier, met)
    else:

        @pl.loop(1, total)
        def _(hop):
            pl.semaphore_signal(
                barrier,
                inc=1,
                device_id=place((my_index + hop) % total),
                device_id_type=pl.DeviceIdType.MESH,
            )

        pl.semaphore_wait(barrier, total - 1)

    line = jnp.zeros((3, s_ref.shape[1], cx, 1, cz), jnp.float32)
    s_ref[:, :, :, PAD - 1 : PAD, :] = line
    s_ref[:, :, :, PAD + cy : PAD + cy + 1, :] = line
    for axis, halo in (("cfd", hx_ref), ("panel", hy_ref)):
        for side, way in enumerate((-1, 1)):

            @pl.when(jnp.logical_not(has[axis, way]))
            def _():
                halo[:, side] = jnp.zeros((3,) + halo.shape[2:], jnp.float32)

    zs_ref[...] = jnp.zeros(zs_ref.shape, jnp.float32)

    def route(buf, axis, way):
        side = 0 if way == 1 else 1
        if axis == "cfd":
            src = s_ref.at[buf, :, cx - 1 if way == 1 else 0, pl.ds(PAD, cy), :]
            dst = hx_ref.at[buf, side]
        elif axis == "panel":
            src = ys_ref.at[buf, 1 - side]
            dst = hy_ref.at[buf, side]
        else:
            src = zs_ref.at[buf]
            dst = zr_ref.at[buf]
        lane = 2 * AXES.index(axis) + (way == 1)
        return pltpu.make_async_remote_copy(
            src_ref=src,
            dst_ref=dst,
            send_sem=send_sem.at[buf, lane],
            recv_sem=recv_sem.at[buf, lane],
            device_id={**me, axis: me[axis] + way},
            device_id_type=pl.DeviceIdType.MESH,
        )

    def send(buf, axes):
        for axis in axes:
            for way in (1, -1):

                @pl.when(has[axis, way])
                def _():
                    route(buf, axis, way).start()

    def settle(buf):
        for axis in AXES:
            for way in (1, -1):

                @pl.when(has[axis, -way])
                def _():
                    route(buf, axis, way).wait_recv()

        for axis in AXES:
            for way in (1, -1):

                @pl.when(has[axis, way])
                def _():
                    route(buf, axis, way).wait_send()

    lane_id = lax.broadcasted_iota(jnp.int32, (cy, cz), 1)
    row_id = lax.broadcasted_iota(jnp.int32, (cy, cz), 0)
    fields = s_ref.shape[1]

    assert fields * cx <= cz

    def rim_lane(value):
        return jnp.where(low, value[:, 0:1], value[:, cz - 1 : cz])

    def collect(packed, x, f, value):
        spot = f * cx + x
        return jnp.where(lane_id == spot, pltpu.roll(value, spot + 1 - me["obs"], 1), packed)

    def pack_sides(buf):
        for f in range(fields):
            for side, row in enumerate((PAD, PAD + cy - 1)):
                ys_ref[buf, side, f] = s_ref[buf, f, :, row, :]

    def blank():
        return jnp.zeros((cy, cz), jnp.float32)

    half = 0.5 * TIME_STEP

    def bulk(src, dst, number):
        packed = blank()
        for x in range(cx):
            visc_h = v_ref[x]
            speed_h = m_ref[x]
            mid, moved, ups, across, along = [], [], {}, {}, []
            for f in range(fields):
                c = s_ref[src, f, x, PAD : PAD + cy, :]
                n = s_ref[src, f, x, PAD + 1 : PAD + cy + 1, :]
                s = s_ref[src, f, x, PAD - 1 : PAD + cy - 1, :]
                u = jnp.where(lane_id == cz - 1, 0.0, pltpu.roll(c, cz - 1, 1))
                d = jnp.where(lane_id == 0, 0.0, pltpu.roll(c, 1, 1))
                if x == 0:
                    dx = sx = s_ref[src, f, x + 1, PAD : PAD + cy, :]
                elif x == cx - 1:
                    sx = s_ref[src, f, x - 1, PAD : PAD + cy, :]
                    dx = -sx
                else:
                    e = s_ref[src, f, x + 1, PAD : PAD + cy, :]
                    w = s_ref[src, f, x - 1, PAD : PAD + cy, :]
                    dx, sx = e - w, e + w
                spread = sx + (n + s) + (u + d) - 6.0 * c
                mid.append(c)
                along.append(dx)
                moved.append(visc_h * spread - speed_h * dx)
                if f in (2, 4):
                    across[f] = n - s
                if f in (3, 4):
                    ups[f] = u - d
            diverge = half * (along[1] + across[2] + ups[3])
            forcing = [diverge, half * along[4], half * across[4], half * ups[4], diverge]
            for f in range(fields):
                value = mid[f] + (moved[f] - forcing[f])
                if number == 1:
                    value = 0.75 * s_ref[0, f, x, PAD : PAD + cy, :] + 0.25 * value
                elif number == 2:
                    value = s_ref[0, f, x, PAD : PAD + cy, :] * (1.0 / 3.0) + (2.0 / 3.0) * value
                s_ref[dst, f, x, PAD : PAD + cy, :] = value
                packed = collect(packed, x, f, value)
        zs_ref[dst] = packed
        pack_sides(dst)

    sub_id = lax.broadcasted_iota(jnp.int32, (8, cz), 0)

    def push(halo, coef, way, normal, scale):
        sent = -way * half * scale
        base = [(scale * coef) * value for value in halo]
        cross = sent * halo[normal]
        base[0] = base[0] + cross
        base[4] = base[4] + cross
        base[normal] = base[normal] + sent * halo[4]
        return base

    def correct(src, dst, number):
        scale = (1.0, 0.25, 2.0 / 3.0)[number]
        south, north = [
            push([hy_ref[src, side, f] for f in range(fields)], vy_ref[side], way, 2, scale)
            for side, way in enumerate((-1, 1))
        ]
        faces = {}
        for x, side, way in ((0, 0, -1), (cx - 1, 1, 1)):
            coef = v_ref[x] - way * m_ref[x]
            faces[x] = push([hx_ref[src, side, f] for f in range(fields)], coef, way, 1, scale)
        spot = lax.broadcasted_iota(jnp.int32, (cx, cz), 1)
        step_id = lax.broadcasted_iota(jnp.int32, (cx, cz), 0)
        end = jnp.where(low, 0, cz - 1)
        sent = jnp.where(low, half * scale, -half * scale)
        held = zr_ref[src]
        cross = jnp.where(
            lane_id < cx,
            pltpu.roll(held, cz - 3 * cx, 1),
            jnp.where(lane_id < 4 * cx, pltpu.roll(held, cz - cx, 1), pltpu.roll(held, cx, 1)),
        )
        crossed = (lane_id < cx) | ((lane_id >= 3 * cx) & (lane_id < 5 * cx))
        fix = (scale * vz_ref[...]) * held + sent * jnp.where(crossed, cross, 0.0)
        tall = jnp.zeros((cy, cz), jnp.float32)
        for x in (0, cx - 1):
            for f in range(fields):
                tall = collect(tall, x, f, faces[x][f])
        rows_out = []
        for own in (south, north):
            wide = jnp.zeros((cx, cz), jnp.float32)
            for f in range(fields):
                wide = jnp.where(spot == step_id + f * cx, rim_lane(own[f]), wide)
            rows_out.append(jnp.sum(wide, axis=0, keepdims=True))
        tall = tall + jnp.where(row_id == 0, rows_out[0], 0.0)
        tall = tall + jnp.where(row_id == cy - 1, rows_out[1], 0.0)
        zs_ref[dst] = zs_ref[dst] + (fix + tall)
        yield "obs"
        turned = jnp.transpose(fix)
        for side, (own, row) in enumerate(((south, 0), (north, cy - 1))):
            for f in range(fields):
                ends = turned[f * cx : (f + 1) * cx, row : row + 1]
                side_fix = own[f] + jnp.where(spot == end, ends, 0.0)
                for x in (0, cx - 1):
                    side_fix = side_fix + jnp.where(step_id == x, faces[x][f][row : row + 1, :], 0.0)
                ys_ref[dst, side, f] = ys_ref[dst, side, f] + side_fix
        yield "panel"
        for place_x, x in enumerate([0, cx - 1] + list(range(1, cx - 1))):
            for f in range(fields):
                rim = [jnp.where(sub_id == 0, south[f][x : x + 1, :], 0.0)]
                if cy > 16:
                    rim.append(jnp.zeros((cy - 16, cz), jnp.float32))
                rim.append(jnp.where(sub_id == 7, north[f][x : x + 1, :], 0.0))
                edge = jnp.where(lane_id == end, fix[:, f * cx + x : f * cx + x + 1], 0.0)
                value = s_ref[dst, f, x, PAD : PAD + cy, :] + (
                    jnp.concatenate(rim, axis=0) + edge
                )
                if x in faces:
                    value = value + faces[x][f]
                s_ref[dst, f, x, PAD : PAD + cy, :] = value
            if place_x == 1:
                yield "cfd"

    cap, groups = cells.shape
    slots = cap * groups

    def mark():
        lane = lax.broadcasted_iota(jnp.int32, (2, cz), 1)

        def body(slot, carry):
            rank, group = lax.rem(slot, cap), lax.div(slot, cap)
            spot = jnp.where(rank < counts[group], lax.rem(cells[rank, group], cz), -1)
            hot_ref[pl.ds(2 * slot, 2), :] = (lane == spot).astype(jnp.float32)
            return carry

        lax.fori_loop(0, slots, body, 0)

    def sample():
        def body(group, carry):
            for rank in range(cap):
                slot = group * cap + rank
                row = lax.div(cells[rank, group], cz)
                for t, f in enumerate((0, 4)):
                    g_ref[pl.ds(2 * slot + t, 1), :] = s_ref[
                        0, f, lax.div(row, cy), pl.ds(PAD + lax.rem(row, cy), 1), :
                    ]
            return carry

        lax.fori_loop(0, groups, body, 0, unroll=min(groups, 8))
        heard = jnp.sum(jnp.where(hot_ref[...] != 0.0, g_ref[...], 0.0), axis=1, keepdims=True)
        heard = heard.astype(jnp.bfloat16).astype(jnp.float32)
        return jnp.broadcast_to(heard, g_ref.shape)

    def parcel_copy(offset):
        where_to = (me["cfd"] * sizes[2] + me["obs"] + offset) % (sizes[0] * sizes[2])
        c, z = where_to // sizes[2], where_to % sizes[2]
        return pltpu.make_async_remote_copy(
            src_ref=parcel_ref.at[z, c],
            dst_ref=w_ref.at[me["obs"] * sizes[0] + me["cfd"]],
            send_sem=w_sem.at[0],
            recv_sem=w_sem.at[1],
            device_id={"cfd": c, "panel": me["panel"], "obs": z},
            device_id_type=pl.DeviceIdType.MESH,
        )

    def result_copy(target):
        block = (target["obs"] * sizes[0] + target["cfd"]) * sizes[1] + target["panel"]
        return pltpu.make_async_remote_copy(
            src_ref=part_ref.at[block],
            dst_ref=gather_ref.at[my_index],
            send_sem=r_sem.at[0],
            recv_sem=r_sem.at[1],
            device_id=target,
            device_id_type=pl.DeviceIdType.MESH,
        )

    def turn(axis, offset):
        moved = me[axis] + offset
        return jnp.where(moved >= span[axis], moved - span[axis], moved)

    loads[0].wait()
    send(0, ("cfd",))
    pack_sides(0)
    send(0, ("panel",))
    packed = blank()
    for x in range(cx):
        for f in range(fields):
            packed = collect(packed, x, f, s_ref[0, f, x, PAD : PAD + cy, :])
    zs_ref[0] = packed
    send(0, ("obs",))
    for load in loads[1:]:
        load.wait()
    m_ref[...] = half * m_ref[...]
    visc_all = TIME_STEP * v_ref[...]
    v_ref[...] = visc_all
    vy_ref[0] = visc_all[:, 0, :]
    vy_ref[1] = visc_all[:, cy - 1, :]
    rims = blank()
    for x in range(cx):
        for f in range(fields):
            rims = collect(rims, x, f, visc_all[x])
    vz_ref[...] = rims

    observers = raw_ref.shape[3]
    parcel_ref[:, :, :, :observers] = raw_ref[...].astype(jnp.float32)
    rest = (raw_ref.shape[2], parcel_ref.shape[3] - observers)
    rest_lane = lax.broadcasted_iota(jnp.int32, rest, 1)
    for z in range(sizes[2]):

        @pl.loop(0, sizes[0])
        def _(c):
            value = jnp.zeros(rest, jnp.int32)
            for b in range(late_bins.shape[1]):
                value = jnp.where(rest_lane == b, late_bins[z, b, c], value)
            parcel_ref[z, c, :, observers:] = value.astype(jnp.float32)

    mark()
    group = sizes[0] * sizes[2]
    share = part_ref.shape[1]
    half_rows = part_ref.shape[0] * share // sizes[2]
    blocks = max(half_rows // 128, 1)
    block_rows = half_rows // blocks
    depth = 2 * slots
    bins = lax.broadcasted_iota(jnp.int32, (depth, part_ref.shape[2]), 1).astype(jnp.float32)

    def prepare():
        w_ref[me["obs"] * sizes[0] + me["cfd"]] = parcel_ref[me["obs"], me["cfd"]]
        whole = w_ref.at[pl.ds(0, group - 1)]
        pltpu.make_async_copy(whole, whole, w_sem.at[1]).wait()
        pltpu.make_async_copy(whole, whole, w_sem.at[0]).wait()
        for h in range(sizes[2]):
            held = slice(h * sizes[0], (h + 1) * sizes[0])
            for b in range(blocks):
                weight = w_ref[held, :, b * block_rows : (b + 1) * block_rows].reshape(depth, block_rows)
                delay = w_ref[held, :, half_rows + b : half_rows + b + 1].reshape(depth, 1)
                late = bins - delay
                spread = jnp.zeros(bins.shape, jnp.float32)
                for k in range(STEPS - 1):
                    spread = jnp.where(late == float(k), sig_ref[k], spread)
                wt_ref[h, b] = jnp.transpose(weight).astype(jnp.bfloat16)
                late_ref[h, b] = late
                early_ref[h, b] = spread

    @pl.loop(0, STEPS)
    def _(step):
        @pl.when(step == STEPS - 1)
        def _():
            @pl.loop(1, sizes[0] * sizes[2])
            def _(offset):
                parcel_copy(offset).start()

        for number in range(3):
            src, dst = number, (number + 1) % 3
            bulk(src, dst, number)
            if number == 2:

                @pl.when(step == STEPS - 1)
                def _():
                    prepare()

            settle(src)
            more = jnp.logical_or(step < STEPS - 1, number < 2)
            for axis in correct(src, dst, number):

                @pl.when(more)
                def _():
                    send(dst, (axis,))

            if number == 2:

                @pl.when(step < STEPS - 1)
                def _():
                    sig_ref[step] = sample()

    final = sample()
    for h in range(sizes[2]):
        for b in range(blocks):
            spread = jnp.where(late_ref[h, b] == float(STEPS - 1), final, early_ref[h, b])
            heard = lax.dot_general(
                wt_ref[h, b],
                spread.astype(jnp.bfloat16),
                (((1,), (0,)), ((), ())),
                preferred_element_type=jnp.float32,
            )
            first = (h * half_rows + b * block_rows) // share
            part_ref[first : first + block_rows // share] = heard.reshape(
                block_rows // share, share, part_ref.shape[2]
            )

    if total <= 64:
        hops = sorted(range(sizes[0]), key=lambda a: (a == 0, min(a, sizes[0] - a)))
        for a in hops:
            places = [(a, b, d) for b in reversed(range(sizes[1])) for d in reversed(range(sizes[2]))]
            for spots in places:
                if any(spots):
                    result_copy({axis: turn(axis, k) for axis, k in zip(AXES, spots)}).start()
    else:

        @pl.loop(1, total)
        def _(offset):
            result_copy(place((my_index + offset) % total)).start()

    flow_out[...] = s_ref[0, :, :, PAD : PAD + cy, :]
    own = (me["obs"] * sizes[0] + me["cfd"]) * sizes[1] + me["panel"]
    gather_ref[my_index] = part_ref[own]

    others = gather_ref.at[pl.ds(0, total - 1)]
    pltpu.make_async_copy(others, others, r_sem.at[1]).wait()
    heard_out[...] = jnp.sum(gather_ref[...], axis=0)

    pltpu.make_async_copy(others, others, r_sem.at[0]).wait()


def per_device(sizes, state, mean_speed, eddy_visc, panel_cell, panel_count, weights, delays):
    fields, cx, cy, cz = state.shape
    slots = panel_cell.shape[3] * panel_cell.shape[4]
    halves, sources, cap, kinds = weights.shape[1:5]
    observers = weights.shape[6]
    blocks = delays.shape[4]
    bins = 128
    width = -(-(observers + blocks) // 128) * 128
    deep = cap * kinds
    weight = weights.reshape(halves, sources, deep, observers)
    delay = delays.reshape(halves, sources, blocks).transpose(0, 2, 1)
    cell = panel_cell.reshape(panel_cell.shape[3:]).transpose(1, 0)
    total = sizes[0] * sizes[1] * sizes[2]
    share = observers // (sizes[0] * sizes[1])
    parts = max(observers // 128, 1)
    anywhere = pl.BlockSpec(memory_space=pl.ANY)
    scalar = pl.BlockSpec(memory_space=pltpu.SMEM)
    flow, heard = pl.pallas_call(
        functools.partial(window_kernel, sizes),
        out_shape=(
            pltpu.VMEM(state.shape, jnp.float32),
            pltpu.VMEM((share, bins), jnp.float32),
        ),
        in_specs=[scalar, scalar, scalar, anywhere, anywhere, anywhere, anywhere],
        out_specs=(pl.BlockSpec(memory_space=pltpu.VMEM),) * 2,
        scratch_shapes=[
            pltpu.VMEM((3, fields, cx, cy + 2 * PAD, cz), jnp.float32),
            pltpu.VMEM((3, 2, fields, cy, cz), jnp.float32),
            pltpu.VMEM((3, 2, fields, cx, cz), jnp.float32),
            pltpu.VMEM((3, 2, fields, cx, cz), jnp.float32),
            pltpu.VMEM((cx, cy, cz), jnp.float32),
            pltpu.VMEM((cx, cy, cz), jnp.float32),
            pltpu.VMEM((2, cx, cz), jnp.float32),
            pltpu.VMEM((cy, cz), jnp.float32),
            pltpu.VMEM((3, cy, cz), jnp.float32),
            pltpu.VMEM((3, cy, cz), jnp.float32),
            pltpu.VMEM((halves, sources, deep, observers), jnp.bfloat16),
            pltpu.VMEM((2 * slots, cz), jnp.float32),
            pltpu.VMEM((2 * slots, cz), jnp.float32),
            pltpu.VMEM((STEPS - 1, 2 * slots, bins), jnp.float32),
            pltpu.VMEM((halves, sources, deep, width), jnp.float32),
            pltpu.VMEM((halves * sources, deep, width), jnp.float32),
            pltpu.VMEM((halves, parts, observers // parts, 2 * slots), jnp.bfloat16),
            pltpu.VMEM((halves, parts, 2 * slots, bins), jnp.float32),
            pltpu.VMEM((halves, parts, 2 * slots, bins), jnp.float32),
            pltpu.VMEM((total, share, bins), jnp.float32),
            pltpu.VMEM((total, share, bins), jnp.float32),
            pltpu.SemaphoreType.DMA((4,)),
            pltpu.SemaphoreType.DMA((3, 6)),
            pltpu.SemaphoreType.DMA((3, 6)),
            pltpu.SemaphoreType.DMA((2,)),
            pltpu.SemaphoreType.DMA((2,)),
        ],
        compiler_params=pltpu.CompilerParams(collective_id=0, has_side_effects=True),
        name="window",
    )(cell, panel_count.reshape(-1), delay, state, mean_speed, eddy_visc, weight)
    return flow, heard[None]


def solution(mesh):
    in_specs = (
        P(None, "cfd", "panel", "obs"),
        P("cfd", "panel", "obs"),
        P("cfd", "panel", "obs"),
        P("cfd", "panel", "obs", None, None),
        P("cfd", "panel", "obs", None),
        P(("cfd", "panel"), None, None, None, None, "obs", None),
        P(("cfd", "panel"), None, None, "obs", None),
    )
    out_specs = (P(None, "cfd", "panel", "obs"), P("obs", ("cfd", "panel"), None))
    sizes = tuple(mesh.shape[axis] for axis in AXES)
    return jax.shard_map(
        functools.partial(per_device, sizes),
        mesh=mesh,
        in_specs=in_specs,
        out_specs=out_specs,
        check_vma=False,
    )
```

```python
import functools

import jax
import jax.numpy as jnp
from jax import lax
from jax.experimental import pallas as pl
from jax.experimental.pallas import tpu as pltpu
from jax.sharding import PartitionSpec as P

STEPS = 4
TIME_STEP = 0.2
PAD = 8
AXES = ("cfd", "panel", "obs")


def window_kernel(
    sizes,
    cells,
    counts,
    late_bins,
    state,
    speed,
    visc,
    weights,
    flow_out,
    heard_out,
    s_ref,
    hx_ref,
    hy_ref,
    ys_ref,
    yb_ref,
    m_ref,
    v_ref,
    vy_ref,
    vz_ref,
    zs_ref,
    zb_ref,
    zr_ref,
    raw_ref,
    g_ref,
    hot_ref,
    sig_ref,
    parcel_ref,
    w_ref,
    wt_ref,
    late_ref,
    early_ref,
    part_ref,
    gather_ref,
    load_sem,
    send_sem,
    recv_sem,
    w_sem,
    r_sem,
):
    span = dict(zip(AXES, sizes))
    cx, cy, cz = speed.shape
    rows = cx * cy
    me = {axis: lax.axis_index(axis) for axis in AXES}
    has = {}
    for axis in AXES:
        has[axis, 1] = me[axis] < span[axis] - 1
        has[axis, -1] = me[axis] > 0
    total = sizes[0] * sizes[1] * sizes[2]
    assert sizes[2] == 2
    low = me["obs"] > 0
    near = sum(sizes) - 3 <= 3 * (STEPS - 1)

    loads = [
        pltpu.make_async_copy(
            state, s_ref.at[0, :, :, pl.ds(PAD, cy), :], load_sem.at[0]
        ),
        pltpu.make_async_copy(speed, m_ref, load_sem.at[1]),
        pltpu.make_async_copy(visc, v_ref, load_sem.at[2]),
        pltpu.make_async_copy(weights, raw_ref, load_sem.at[3]),
    ]
    for load in loads:
        load.start()

    def place(index):
        return {
            "cfd": index // (sizes[1] * sizes[2]),
            "panel": (index // sizes[2]) % sizes[1],
            "obs": index % sizes[2],
        }

    my_index = (me["cfd"] * sizes[1] + me["panel"]) * sizes[2] + me["obs"]
    barrier = pltpu.get_barrier_semaphore()
    if near:
        met = jnp.int32(0)
        for axis in AXES:
            for way in (1, -1):

                @pl.when(has[axis, way])
                def _():
                    pl.semaphore_signal(
                        barrier,
                        inc=1,
                        device_id={**me, axis: me[axis] + way},
                        device_id_type=pl.DeviceIdType.MESH,
                    )

                met = met + has[axis, way].astype(jnp.int32)
        pl.semaphore_wait(barrier, met)
    else:

        @pl.loop(1, total)
        def _(hop):
            pl.semaphore_signal(
                barrier,
                inc=1,
                device_id=place((my_index + hop) % total),
                device_id_type=pl.DeviceIdType.MESH,
            )

        pl.semaphore_wait(barrier, total - 1)

    line = jnp.zeros((3, s_ref.shape[1], cx, 1, cz), jnp.float32)
    s_ref[:, :, :, PAD - 1 : PAD, :] = line
    s_ref[:, :, :, PAD + cy : PAD + cy + 1, :] = line
    for axis, halo in (("cfd", hx_ref), ("panel", hy_ref)):
        for side, way in enumerate((-1, 1)):

            @pl.when(jnp.logical_not(has[axis, way]))
            def _():
                halo[:, side] = jnp.zeros((3,) + halo.shape[2:], halo.dtype)


    def route(buf, axis, way):
        side = 0 if way == 1 else 1
        if axis == "cfd":
            src = s_ref.at[buf, :, cx - 1 if way == 1 else 0, pl.ds(PAD, cy), :]
            dst = hx_ref.at[buf, side]
        elif axis == "panel":
            src = yb_ref.at[buf, 1 - side]
            dst = hy_ref.at[buf, side]
        else:
            src = zb_ref.at[buf]
            dst = zr_ref.at[buf]
        lane = 2 * AXES.index(axis) + (way == 1)
        return pltpu.make_async_remote_copy(
            src_ref=src,
            dst_ref=dst,
            send_sem=send_sem.at[buf, lane],
            recv_sem=recv_sem.at[buf, lane],
            device_id={**me, axis: me[axis] + way},
            device_id_type=pl.DeviceIdType.MESH,
        )

    def send(buf, axes):
        for axis in axes:
            for way in (1, -1):

                @pl.when(has[axis, way])
                def _():
                    route(buf, axis, way).start()

    def settle(buf):
        for axis in AXES:
            for way in (1, -1):

                @pl.when(has[axis, -way])
                def _():
                    route(buf, axis, way).wait_recv()

        for axis in AXES:
            for way in (1, -1):

                @pl.when(has[axis, way])
                def _():
                    route(buf, axis, way).wait_send()

    lane_id = lax.broadcasted_iota(jnp.int32, (cy, cz), 1)
    row_id = lax.broadcasted_iota(jnp.int32, (cy, cz), 0)
    fields = s_ref.shape[1]

    assert fields * cx <= cz

    def rim_lane(value):
        return jnp.where(low, value[:, 0:1], value[:, cz - 1 : cz])

    def collect(packed, x, f, value):
        spot = f * cx + x
        return jnp.where(lane_id == spot, pltpu.roll(value, spot + 1 - me["obs"], 1), packed)

    def pack_sides(buf):
        for f in range(fields):
            for side, row in enumerate((PAD, PAD + cy - 1)):
                ys_ref[side, f] = s_ref[buf, f, :, row, :]

    def put_side(buf, side, parts):
        rest = jnp.zeros((yb_ref.shape[2] - fields * cx, cz), jnp.float32)
        tall = jnp.concatenate(parts + ([rest] if rest.shape[0] else []), axis=0)
        yb_ref[buf, side] = tall.astype(yb_ref.dtype)

    def fill_sides(buf):
        for side, row in enumerate((PAD, PAD + cy - 1)):
            put_side(buf, side, [s_ref[buf, f, :, row, :] for f in range(fields)])

    def put_rim(buf, value):
        zb_ref[buf] = value.astype(zb_ref.dtype)

    def blank():
        return jnp.zeros((cy, cz), jnp.float32)

    half = 0.5 * TIME_STEP

    def bulk(src, dst, number):
        packed = blank()
        for x in range(cx):
            visc_h = v_ref[x]
            speed_h = m_ref[x]
            mid, moved, ups, across, along = [], [], {}, {}, []
            for f in range(fields):
                c = s_ref[src, f, x, PAD : PAD + cy, :]
                n = s_ref[src, f, x, PAD + 1 : PAD + cy + 1, :]
                s = s_ref[src, f, x, PAD - 1 : PAD + cy - 1, :]
                u = jnp.where(lane_id == cz - 1, 0.0, pltpu.roll(c, cz - 1, 1))
                d = jnp.where(lane_id == 0, 0.0, pltpu.roll(c, 1, 1))
                if x == 0:
                    dx = sx = s_ref[src, f, x + 1, PAD : PAD + cy, :]
                elif x == cx - 1:
                    sx = s_ref[src, f, x - 1, PAD : PAD + cy, :]
                    dx = -sx
                else:
                    e = s_ref[src, f, x + 1, PAD : PAD + cy, :]
                    w = s_ref[src, f, x - 1, PAD : PAD + cy, :]
                    dx, sx = e - w, e + w
                spread = sx + (n + s) + (u + d) - 6.0 * c
                mid.append(c)
                along.append(dx)
                moved.append(visc_h * spread - speed_h * dx)
                if f in (2, 4):
                    across[f] = n - s
                if f in (3, 4):
                    ups[f] = u - d
            diverge = half * (along[1] + across[2] + ups[3])
            forcing = [diverge, half * along[4], half * across[4], half * ups[4], diverge]
            for f in range(fields):
                value = mid[f] + (moved[f] - forcing[f])
                if number == 1:
                    value = 0.75 * s_ref[0, f, x, PAD : PAD + cy, :] + 0.25 * value
                elif number == 2:
                    value = s_ref[0, f, x, PAD : PAD + cy, :] * (1.0 / 3.0) + (2.0 / 3.0) * value
                s_ref[dst, f, x, PAD : PAD + cy, :] = value
                packed = collect(packed, x, f, value)
        zs_ref[...] = packed
        pack_sides(dst)

    sub_id = lax.broadcasted_iota(jnp.int32, (8, cz), 0)

    def push(halo, coef, way, normal, scale):
        sent = -way * half * scale
        base = [(scale * coef) * value for value in halo]
        cross = sent * halo[normal]
        base[0] = base[0] + cross
        base[4] = base[4] + cross
        base[normal] = base[normal] + sent * halo[4]
        return base

    def split(tall):
        return [tall[f * cx : (f + 1) * cx] for f in range(fields)]

    def correct(src, dst, number):
        scale = (1.0, 0.25, 2.0 / 3.0)[number]
        south, north = [
            push(split(hy_ref[src, side].astype(jnp.float32)), vy_ref[side], way, 2, scale)
            for side, way in enumerate((-1, 1))
        ]
        faces = {}
        for x, side, way in ((0, 0, -1), (cx - 1, 1, 1)):
            coef = v_ref[x] - way * m_ref[x]
            faces[x] = push([hx_ref[src, side, f] for f in range(fields)], coef, way, 1, scale)
        spot = lax.broadcasted_iota(jnp.int32, (cx, cz), 1)
        step_id = lax.broadcasted_iota(jnp.int32, (cx, cz), 0)
        end = jnp.where(low, 0, cz - 1)
        sent = jnp.where(low, half * scale, -half * scale)
        held = zr_ref[src].astype(jnp.float32)
        cross = jnp.where(
            lane_id < cx,
            pltpu.roll(held, cz - 3 * cx, 1),
            jnp.where(lane_id < 4 * cx, pltpu.roll(held, cz - cx, 1), pltpu.roll(held, cx, 1)),
        )
        crossed = (lane_id < cx) | ((lane_id >= 3 * cx) & (lane_id < 5 * cx))
        fix = (scale * vz_ref[...]) * held + sent * jnp.where(crossed, cross, 0.0)
        turned = jnp.transpose(fix)
        for side, (own, row) in enumerate(((south, 0), (north, cy - 1))):
            parts = []
            for f in range(fields):
                ends = turned[f * cx : (f + 1) * cx, row : row + 1]
                side_fix = own[f] + jnp.where(spot == end, ends, 0.0)
                for x in (0, cx - 1):
                    side_fix = side_fix + jnp.where(step_id == x, faces[x][f][row : row + 1, :], 0.0)
                parts.append(ys_ref[side, f] + side_fix)
            put_side(dst, side, parts)
        yield "panel"
        tall = jnp.zeros((cy, cz), jnp.float32)
        for x in (0, cx - 1):
            for f in range(fields):
                tall = collect(tall, x, f, faces[x][f])
        rows_out = []
        for own in (south, north):
            wide = jnp.zeros((cx, cz), jnp.float32)
            for f in range(fields):
                wide = jnp.where(spot == step_id + f * cx, rim_lane(own[f]), wide)
            rows_out.append(jnp.sum(wide, axis=0, keepdims=True))
        tall = tall + jnp.where(row_id == 0, rows_out[0], 0.0)
        tall = tall + jnp.where(row_id == cy - 1, rows_out[1], 0.0)
        put_rim(dst, zs_ref[...] + (fix + tall))
        yield "obs"
        for place_x, x in enumerate([0, cx - 1] + list(range(1, cx - 1))):
            for f in range(fields):
                rim = [jnp.where(sub_id == 0, south[f][x : x + 1, :], 0.0)]
                if cy > 16:
                    rim.append(jnp.zeros((cy - 16, cz), jnp.float32))
                rim.append(jnp.where(sub_id == 7, north[f][x : x + 1, :], 0.0))
                edge = jnp.where(lane_id == end, fix[:, f * cx + x : f * cx + x + 1], 0.0)
                value = s_ref[dst, f, x, PAD : PAD + cy, :] + (
                    jnp.concatenate(rim, axis=0) + edge
                )
                if x in faces:
                    value = value + faces[x][f]
                s_ref[dst, f, x, PAD : PAD + cy, :] = value
            if place_x == 1:
                yield "cfd"

    cap, groups = cells.shape
    slots = cap * groups

    def mark():
        lane = lax.broadcasted_iota(jnp.int32, (2, cz), 1)

        def body(slot, carry):
            rank, group = lax.rem(slot, cap), lax.div(slot, cap)
            spot = jnp.where(rank < counts[group], lax.rem(cells[rank, group], cz), -1)
            hot_ref[pl.ds(2 * slot, 2), :] = (lane == spot).astype(jnp.float32)
            return carry

        lax.fori_loop(0, slots, body, 0)

    def sample():
        def body(group, carry):
            for rank in range(cap):
                slot = group * cap + rank
                row = lax.div(cells[rank, group], cz)
                for t, f in enumerate((0, 4)):
                    g_ref[pl.ds(2 * slot + t, 1), :] = s_ref[
                        0, f, lax.div(row, cy), pl.ds(PAD + lax.rem(row, cy), 1), :
                    ]
            return carry

        lax.fori_loop(0, groups, body, 0, unroll=min(groups, 8))
        heard = jnp.sum(jnp.where(hot_ref[...] != 0.0, g_ref[...], 0.0), axis=1, keepdims=True)
        heard = heard.astype(jnp.bfloat16).astype(jnp.float32)
        return jnp.broadcast_to(heard, g_ref.shape)

    def parcel_copy(offset):
        where_to = (me["cfd"] * sizes[2] + me["obs"] + offset) % (sizes[0] * sizes[2])
        c, z = where_to // sizes[2], where_to % sizes[2]
        return pltpu.make_async_remote_copy(
            src_ref=parcel_ref.at[z, c],
            dst_ref=w_ref.at[me["obs"] * sizes[0] + me["cfd"]],
            send_sem=w_sem.at[0],
            recv_sem=w_sem.at[1],
            device_id={"cfd": c, "panel": me["panel"], "obs": z},
            device_id_type=pl.DeviceIdType.MESH,
        )

    def result_copy(target):
        block = (target["obs"] * sizes[0] + target["cfd"]) * sizes[1] + target["panel"]
        return pltpu.make_async_remote_copy(
            src_ref=part_ref.at[block],
            dst_ref=gather_ref.at[my_index],
            send_sem=r_sem.at[0],
            recv_sem=r_sem.at[1],
            device_id=target,
            device_id_type=pl.DeviceIdType.MESH,
        )

    def turn(axis, offset):
        moved = me[axis] + offset
        return jnp.where(moved >= span[axis], moved - span[axis], moved)

    loads[0].wait()
    fill_sides(0)
    packed = blank()
    for x in range(cx):
        for f in range(fields):
            packed = collect(packed, x, f, s_ref[0, f, x, PAD : PAD + cy, :])
    put_rim(0, packed)
    send(0, ("panel", "obs", "cfd"))
    for load in loads[1:]:
        load.wait()
    m_ref[...] = half * m_ref[...]
    visc_all = TIME_STEP * v_ref[...]
    v_ref[...] = visc_all
    vy_ref[0] = visc_all[:, 0, :]
    vy_ref[1] = visc_all[:, cy - 1, :]
    rims = blank()
    for x in range(cx):
        for f in range(fields):
            rims = collect(rims, x, f, visc_all[x])
    vz_ref[...] = rims

    observers = raw_ref.shape[3]
    parcel_ref[:, :, :, :observers] = raw_ref[...].astype(jnp.float32)
    rest = (raw_ref.shape[2], parcel_ref.shape[3] - observers)
    rest_lane = lax.broadcasted_iota(jnp.int32, rest, 1)
    for z in range(sizes[2]):

        @pl.loop(0, sizes[0])
        def _(c):
            value = jnp.zeros(rest, jnp.int32)
            for b in range(late_bins.shape[1]):
                value = jnp.where(rest_lane == b, late_bins[z, b, c], value)
            parcel_ref[z, c, :, observers:] = value.astype(jnp.float32)

    mark()
    group = sizes[0] * sizes[2]
    share = part_ref.shape[1]
    half_rows = part_ref.shape[0] * share // sizes[2]
    blocks = max(half_rows // 128, 1)
    block_rows = half_rows // blocks
    depth = 2 * slots
    bins = lax.broadcasted_iota(jnp.int32, (depth, part_ref.shape[2]), 1).astype(jnp.float32)

    def prepare():
        w_ref[me["obs"] * sizes[0] + me["cfd"]] = parcel_ref[me["obs"], me["cfd"]]
        whole = w_ref.at[pl.ds(0, group - 1)]
        pltpu.make_async_copy(whole, whole, w_sem.at[1]).wait()
        pltpu.make_async_copy(whole, whole, w_sem.at[0]).wait()
        for h in range(sizes[2]):
            held = slice(h * sizes[0], (h + 1) * sizes[0])
            for b in range(blocks):
                weight = w_ref[held, :, b * block_rows : (b + 1) * block_rows].reshape(depth, block_rows)
                delay = w_ref[held, :, half_rows + b : half_rows + b + 1].reshape(depth, 1)
                late = bins - delay
                spread = jnp.zeros(bins.shape, jnp.float32)
                for k in range(STEPS - 1):
                    spread = jnp.where(late == float(k), sig_ref[k], spread)
                wt_ref[h, b] = jnp.transpose(weight).astype(jnp.bfloat16)
                late_ref[h, b] = late
                early_ref[h, b] = spread

    @pl.loop(0, STEPS)
    def _(step):
        @pl.when(step == STEPS - 1)
        def _():
            @pl.loop(1, sizes[0] * sizes[2])
            def _(offset):
                parcel_copy(offset).start()

        for number in range(3):
            src, dst = number, (number + 1) % 3
            bulk(src, dst, number)
            if number == 2:

                @pl.when(step == STEPS - 1)
                def _():
                    prepare()

            settle(src)
            more = jnp.logical_or(step < STEPS - 1, number < 2)
            for axes in correct(src, dst, number):
                axes = axes if isinstance(axes, tuple) else (axes,)

                @pl.when(more)
                def _():
                    send(dst, axes)

            if number == 2:

                @pl.when(step < STEPS - 1)
                def _():
                    sig_ref[step] = sample()

    final = sample()
    for h in range(sizes[2]):
        for b in range(blocks):
            spread = jnp.where(late_ref[h, b] == float(STEPS - 1), final, early_ref[h, b])
            heard = lax.dot_general(
                wt_ref[h, b],
                spread.astype(jnp.bfloat16),
                (((1,), (0,)), ((), ())),
                preferred_element_type=jnp.float32,
            )
            first = (h * half_rows + b * block_rows) // share
            part_ref[first : first + block_rows // share] = heard.reshape(
                block_rows // share, share, part_ref.shape[2]
            )

    if total <= 64:
        hops = sorted(range(sizes[0]), key=lambda a: (a == 0, min(a, sizes[0] - a)))
        for a in hops:
            places = [(a, b, d) for b in reversed(range(sizes[1])) for d in reversed(range(sizes[2]))]
            for spots in places:
                if any(spots):
                    result_copy({axis: turn(axis, k) for axis, k in zip(AXES, spots)}).start()
    else:

        @pl.loop(1, total)
        def _(offset):
            result_copy(place((my_index + offset) % total)).start()

    flow_out[...] = s_ref[0, :, :, PAD : PAD + cy, :]
    own = (me["obs"] * sizes[0] + me["cfd"]) * sizes[1] + me["panel"]
    gather_ref[my_index] = part_ref[own]

    others = gather_ref.at[pl.ds(0, total - 1)]
    pltpu.make_async_copy(others, others, r_sem.at[1]).wait()
    heard_out[...] = jnp.sum(gather_ref[...], axis=0)

    pltpu.make_async_copy(others, others, r_sem.at[0]).wait()


def per_device(sizes, state, mean_speed, eddy_visc, panel_cell, panel_count, weights, delays):
    fields, cx, cy, cz = state.shape
    slots = panel_cell.shape[3] * panel_cell.shape[4]
    halves, sources, cap, kinds = weights.shape[1:5]
    observers = weights.shape[6]
    blocks = delays.shape[4]
    bins = 128
    width = -(-(observers + blocks) // 128) * 128
    deep = cap * kinds
    weight = weights.reshape(halves, sources, deep, observers)
    delay = delays.reshape(halves, sources, blocks).transpose(0, 2, 1)
    cell = panel_cell.reshape(panel_cell.shape[3:]).transpose(1, 0)
    total = sizes[0] * sizes[1] * sizes[2]
    share = observers // (sizes[0] * sizes[1])
    parts = max(observers // 128, 1)
    tall = -(-fields * cx // 16) * 16
    anywhere = pl.BlockSpec(memory_space=pl.ANY)
    scalar = pl.BlockSpec(memory_space=pltpu.SMEM)
    flow, heard = pl.pallas_call(
        functools.partial(window_kernel, sizes),
        out_shape=(
            pltpu.VMEM(state.shape, jnp.float32),
            pltpu.VMEM((share, bins), jnp.float32),
        ),
        in_specs=[scalar, scalar, scalar, anywhere, anywhere, anywhere, anywhere],
        out_specs=(pl.BlockSpec(memory_space=pltpu.VMEM),) * 2,
        scratch_shapes=[
            pltpu.VMEM((3, fields, cx, cy + 2 * PAD, cz), jnp.float32),
            pltpu.VMEM((3, 2, fields, cy, cz), jnp.float32),
            pltpu.VMEM((3, 2, tall, cz), jnp.bfloat16),
            pltpu.VMEM((2, fields, cx, cz), jnp.float32),
            pltpu.VMEM((3, 2, tall, cz), jnp.bfloat16),
            pltpu.VMEM((cx, cy, cz), jnp.float32),
            pltpu.VMEM((cx, cy, cz), jnp.float32),
            pltpu.VMEM((2, cx, cz), jnp.float32),
            pltpu.VMEM((cy, cz), jnp.float32),
            pltpu.VMEM((cy, cz), jnp.float32),
            pltpu.VMEM((3, cy, cz), jnp.bfloat16),
            pltpu.VMEM((3, cy, cz), jnp.bfloat16),
            pltpu.VMEM((halves, sources, deep, observers), jnp.bfloat16),
            pltpu.VMEM((2 * slots, cz), jnp.float32),
            pltpu.VMEM((2 * slots, cz), jnp.float32),
            pltpu.VMEM((STEPS - 1, 2 * slots, bins), jnp.float32),
            pltpu.VMEM((halves, sources, deep, width), jnp.float32),
            pltpu.VMEM((halves * sources, deep, width), jnp.float32),
            pltpu.VMEM((halves, parts, observers // parts, 2 * slots), jnp.bfloat16),
            pltpu.VMEM((halves, parts, 2 * slots, bins), jnp.float32),
            pltpu.VMEM((halves, parts, 2 * slots, bins), jnp.float32),
            pltpu.VMEM((total, share, bins), jnp.float32),
            pltpu.VMEM((total, share, bins), jnp.float32),
            pltpu.SemaphoreType.DMA((4,)),
            pltpu.SemaphoreType.DMA((3, 6)),
            pltpu.SemaphoreType.DMA((3, 6)),
            pltpu.SemaphoreType.DMA((2,)),
            pltpu.SemaphoreType.DMA((2,)),
        ],
        compiler_params=pltpu.CompilerParams(collective_id=0, has_side_effects=True),
        name="window",
    )(cell, panel_count.reshape(-1), delay, state, mean_speed, eddy_visc, weight)
    return flow, heard[None]


def solution(mesh):
    in_specs = (
        P(None, "cfd", "panel", "obs"),
        P("cfd", "panel", "obs"),
        P("cfd", "panel", "obs"),
        P("cfd", "panel", "obs", None, None),
        P("cfd", "panel", "obs", None),
        P(("cfd", "panel"), None, None, None, None, "obs", None),
        P(("cfd", "panel"), None, None, "obs", None),
    )
    out_specs = (P(None, "cfd", "panel", "obs"), P("obs", ("cfd", "panel"), None))
    sizes = tuple(mesh.shape[axis] for axis in AXES)
    return jax.shard_map(
        functools.partial(per_device, sizes),
        mesh=mesh,
        in_specs=in_specs,
        out_specs=out_specs,
        check_vma=False,
    )
```
